512 devices in a mesh: rows: 64 (over z, x), cols: 8 (over y, core).
Axes of the slice: x: 4, y: 4, z: 16, core: 2. Of those that a mesh axis runs over, the one named last changes fastest.
Arguments:
- descriptors: bfloat16 [65536, 512], P('rows'), may hold values from -17 to 17, as said below
- sparse_points: bfloat16 [8192, 512], P('cols'), may hold values from -0.25 to 0.25
Outputs:
- q_factor: float32 [65536, 256], P('rows')
- r_rows: float32 [256, 8192], P(None, 'cols')
- trailing: bfloat16 [65536, 8192], P('rows', 'cols')
The draws below stay inside these ranges and needn't reach their ends.
Inputs may be any that keep to these rules, and one draw needn't show every extreme that they name: `descriptors`: each row is a random vector times a positive scale of its own.
All inputs are finite; a program needn't handle non-finite values.
Results may differ from the reference program's by a relative error of at most 0.001.
Values may be sent and summed in bfloat16 or wider, within the bound.
No kernel may reach another device: no remote copies, remote signals or barrier semaphores. Data moves between devices by JAX's collectives and lax.ppermute only.
A program may use at most 64 MiB of HBM per device.

```python
import math
import jax
import jax.numpy as jnp
from jax import lax

DW = 512
COL_DEV = 1024
PANEL = 128
NROWS = 65536
SPARSE = 8192


def draw_descriptors(key, part):
    key_values = jax.random.fold_in(key, 11)
    key_scales = jax.random.fold_in(key, 23)
    position = jnp.arange(NROWS, dtype=jnp.float32) / NROWS
    rising = ((1.0 + 2.0 * position) ** 0.25)[:, None]
    values = jax.random.truncated_normal(key_values, -4.0, 4.0, (NROWS, DW), jnp.float32)
    spread = jnp.exp(0.5 * jax.random.uniform(key_scales, (NROWS, 1), jnp.float32, 0.0, math.log(10.0)))
    return (values * spread * rising).astype(jnp.bfloat16)


def steps_of(stream_key, shape, split, least, top_value):
    gain, own = 1.0, jax.random.fold_in(stream_key, 6)
    for axis_at, parts in split:
        steps = jnp.exp(jax.random.uniform(jax.random.fold_in(own, axis_at), (parts,), jnp.float32, least / len(split), top_value / len(split)))
        gain = gain * jnp.repeat(steps, shape[axis_at] // parts).reshape([-1 if axis == axis_at else 1 for axis in range(len(shape))])
    return gain


def gaussian(rng, extent, scale, reach, shards=(), kind=jnp.bfloat16):
    result = jax.random.normal(rng, extent, jnp.float32) * scale
    if len(shards) > 0:
        result = steps_of(rng, extent, shards, -0.22, 0.18) * result
    return jnp.clip(result, min=-reach, max=reach).astype(kind)


def setup_inputs(seed: int = 0) -> dict:
    streams_of = jax.random.split(jax.random.key(seed), 3)
    return {
        "descriptors": draw_descriptors(jax.random.fold_in(streams_of[2], 71), 0),
        "sparse_points": gaussian(streams_of[1], (SPARSE, DW), DW ** -0.5, 0.25, ((0, 8),)),
    }


HIGHEST_PRECISION = lax.Precision.HIGHEST

def factor_panel(panel):
    gram_matrix = jnp.dot(panel.T.astype(jnp.float32), panel.astype(jnp.float32), precision=HIGHEST_PRECISION, preferred_element_type=jnp.float32) / NROWS
    lower = jnp.linalg.cholesky(gram_matrix)
    q_transposed = lax.linalg.triangular_solve(lower, panel.T, left_side=True, lower=True)
    return q_transposed.T

def reference(descriptors, sparse_points):
    inner_dots = jnp.dot(descriptors.astype(jnp.float32), sparse_points.T.astype(jnp.float32), preferred_element_type=jnp.float32)
    kernel = inner_dots * inner_dots
    q_one = factor_panel(kernel[:, :PANEL])
    r_one = jnp.dot(q_one.T.astype(jnp.float32), kernel.astype(jnp.float32), precision=HIGHEST_PRECISION, preferred_element_type=jnp.float32) / NROWS
    updated = kernel - jnp.dot(q_one.astype(jnp.float32), r_one.astype(jnp.float32), precision=HIGHEST_PRECISION, preferred_element_type=jnp.float32)
    q_two = factor_panel(updated[:, COL_DEV:COL_DEV + PANEL])
    r_two = jnp.dot(q_two.T.astype(jnp.float32), updated.astype(jnp.float32), precision=HIGHEST_PRECISION, preferred_element_type=jnp.float32) / NROWS
    trailing = updated - jnp.dot(q_two.astype(jnp.float32), r_two.astype(jnp.float32), precision=HIGHEST_PRECISION, preferred_element_type=jnp.float32)
    q_factor = jnp.concatenate([q_one, q_two], axis=1)
    r_rows = jnp.concatenate([r_one, r_two], axis=0)
    return (q_factor, r_rows, trailing.astype(jnp.bfloat16))
```

```python
import functools

import jax
import jax.numpy as jnp
from jax import lax
from jax.experimental import pallas as pl
from jax.experimental.pallas import tpu as pltpu
from jax.sharding import Mesh, PartitionSpec as P

PANEL = 128
BOTH = 2 * PANEL
F32 = jnp.float32
BF16 = jnp.bfloat16
NT = (((1,), (1,)), ((), ()))
NN = (((1,), (0,)), ((), ()))
TN = (((0,), (0,)), ((), ()))


def split(value):
    high = value.astype(BF16)
    low = (value - high.astype(F32)).astype(BF16)
    return high, low


def dot(first, second, dims):
    return lax.dot_general(first, second, dims, preferred_element_type=F32)


def dot_split(first, second, dims):
    return (
        dot(first[0], second[1], dims)
        + dot(first[1], second[0], dims)
        + dot(first[0], second[0], dims)
    )


def dot_full(first, second, dims):
    return lax.dot_general(
        first, second, dims, precision=lax.Precision.HIGHEST, preferred_element_type=F32
    )


def square(value):
    return value * value


def cholesky_inverse(matrix):
    slabs = PANEL // 8
    lanes = lax.broadcasted_iota(jnp.int32, (8, PANEL), 1)
    sublanes = lax.broadcasted_iota(jnp.int32, (8, PANEL), 0)
    left = [matrix[8 * s : 8 * s + 8, :] for s in range(slabs)]
    right = [(lanes == sublanes + 8 * s).astype(F32) for s in range(slabs)]
    for k in range(PANEL):
        own, at = divmod(k, 8)
        row = left[own][at : at + 1, :]
        scale = lax.rsqrt(jnp.broadcast_to(row[:, k : k + 1], (1, PANEL)))
        row = jnp.broadcast_to(row * scale, (8, PANEL))
        made = jnp.broadcast_to(right[own][at : at + 1, :] * scale, (8, PANEL))
        scale = jnp.broadcast_to(scale, (8, PANEL))
        for s in range(own, slabs):
            factor = jnp.broadcast_to(left[s][:, k : k + 1], (8, PANEL)) * scale
            if s == own:
                factor = jnp.where(sublanes > at, factor, 0.0)
            left[s] = left[s] - factor * row
            kept = right[s] - factor * made
            right[s] = jnp.where(sublanes == at, made, kept) if s == own else kept
    return jnp.concatenate(right, axis=0)


def gather_kernel(scale, rows_ref, points_ref, panel_ref, sums_ref, high_ref, low_ref):
    tile = pl.program_id(0)

    @pl.when(tile == 0)
    def _():
        panels = square(dot(panel_ref[...], rows_ref[...], NT))
        high, low = split(panels)
        high_ref[...] = high
        low_ref[...] = low
        sums = dot_split((high, low), (high, low), NT) * scale
        sums_ref[0] = sums[:, :PANEL]
        sums_ref[1] = sums[:, PANEL:]

    @pl.when(tile > 0)
    def _():
        kernel = split(square(dot(points_ref[...], rows_ref[...], NT)))
        sums = dot_split((high_ref[...], low_ref[...]), kernel, NT) * scale
        sums_ref[0] = sums[:, :PANEL]
        sums_ref[1] = sums[:, PANEL:]


def apply_kernel(
    gram_ref, sums_ref, rows_ref, points_ref, panel_ref, q_ref, r_ref, out_ref,
    inverse_ref, high_ref, low_ref,
):
    @pl.when(pl.program_id(0) == 0)
    def _():
        gram = jnp.concatenate([gram_ref[0], gram_ref[1]], axis=1)
        first = cholesky_inverse(gram[:PANEL, :PANEL])
        lower = dot_full(gram[PANEL:, :PANEL], first, NT)
        second = cholesky_inverse(gram[PANEL:, PANEL:] - dot_full(lower, lower, NT))
        corner = -dot_full(second, dot_full(lower, first, NN), NN)
        inverse_ref[:PANEL, :PANEL] = first
        inverse_ref[:PANEL, PANEL:] = jnp.zeros_like(first)
        inverse_ref[PANEL:, :PANEL] = corner
        inverse_ref[PANEL:, PANEL:] = second
        panels = split(square(dot(rows_ref[...], panel_ref[...], NT)))
        high_ref[...] = panels[0]
        low_ref[...] = panels[1]
        q_ref[...] = dot_split(panels, split(inverse_ref[...]), NT)

    sums = jnp.concatenate([sums_ref[0], sums_ref[1]], axis=1)
    r_tile = dot_full(inverse_ref[...], sums, NN)
    r_ref[...] = r_tile
    weights = split(dot_full(inverse_ref[...], r_tile, TN))
    kernel = square(dot(rows_ref[...], points_ref[...], NT))
    out = kernel - dot_split((high_ref[...], low_ref[...]), weights, NN)
    out_ref[...] = out.astype(BF16)


def exchange(value, axis, count):
    parts = value.reshape(count, value.shape[0] // count, PANEL)
    return jnp.sum(lax.all_to_all(parts, axis, 0, 0), axis=0)


def collect(value, axis, count):
    copies = jnp.broadcast_to(value[None], (count,) + value.shape)
    return lax.all_to_all(copies, axis, 0, 0).reshape(count * value.shape[0], PANEL)


def on_device(sizes, descriptors, points):
    rows, width = descriptors.shape
    columns = points.shape[0]
    tiles = columns // BOTH
    total_rows = rows * sizes["z"] * sizes["x"]

    mine = jnp.broadcast_to(points[None, :PANEL], (sizes["y"], PANEL, width))
    mine = lax.all_to_all(mine, "y", 0, 0)[0]
    other = lax.ppermute(mine, "c", [(0, 1), (1, 0)])
    even = lax.axis_index("c") == 0
    panel = jnp.concatenate([jnp.where(even, mine, other), jnp.where(even, other, mine)], axis=0)

    rows_spec = pl.BlockSpec((rows, width), lambda t: (0, 0))
    panel_spec = pl.BlockSpec((BOTH, width), lambda t: (0, 0))
    sums = pl.pallas_call(
        functools.partial(gather_kernel, 1.0 / total_rows),
        grid=(tiles + 1,),
        in_specs=[
            rows_spec,
            pl.BlockSpec((BOTH, width), lambda t: (jnp.maximum(t - 1, 0), 0)),
            panel_spec,
        ],
        out_specs=pl.BlockSpec((2, BOTH, PANEL), lambda t: (t, 0, 0)),
        out_shape=jax.ShapeDtypeStruct((2 * tiles + 2, BOTH, PANEL), F32),
        scratch_shapes=[pltpu.VMEM((BOTH, rows), BF16)] * 2,
        name="gather",
    )(descriptors, points, panel)

    sums = sums.reshape(-1, PANEL)
    sums = exchange(sums, "x", sizes["x"])
    sums = exchange(sums, "z", sizes["z"])
    sums = collect(sums, "z", sizes["z"])
    sums = collect(sums, "x", sizes["x"])
    sums = sums.reshape(2 * tiles + 2, BOTH, PANEL)

    return pl.pallas_call(
        apply_kernel,
        grid=(tiles,),
        in_specs=[
            pl.BlockSpec((2, BOTH, PANEL), lambda t: (0, 0, 0)),
            pl.BlockSpec((2, BOTH, PANEL), lambda t: (t + 1, 0, 0)),
            rows_spec,
            pl.BlockSpec((BOTH, width), lambda t: (t, 0)),
            panel_spec,
        ],
        out_specs=(
            pl.BlockSpec((rows, BOTH), lambda t: (0, 0)),
            pl.BlockSpec((BOTH, BOTH), lambda t: (0, t)),
            pl.BlockSpec((rows, BOTH), lambda t: (0, t)),
        ),
        out_shape=(
            jax.ShapeDtypeStruct((rows, BOTH), F32),
            jax.ShapeDtypeStruct((BOTH, columns), F32),
            jax.ShapeDtypeStruct((rows, columns), BF16),
        ),
        scratch_shapes=[
            pltpu.VMEM((BOTH, BOTH), F32),
            pltpu.VMEM((rows, BOTH), BF16),
            pltpu.VMEM((rows, BOTH), BF16),
        ],
        name="apply",
    )(sums, sums, descriptors, points, panel)


def solution(mesh):
    names = ("z", "x", "y", "c")
    fine = Mesh(mesh.devices.reshape(16, 4, 4, 2), names)
    return jax.shard_map(
        functools.partial(on_device, dict(zip(names, fine.devices.shape))),
        mesh=fine,
        in_specs=(P(("z", "x"), None), P(("y", "c"), None)),
        out_specs=(P(("z", "x"), None), P(None, ("y", "c")), P(("z", "x"), ("y", "c"))),
        check_vma=False,
    )
```

```python
import functools

import jax
import jax.numpy as jnp
from jax import lax
from jax.experimental import pallas as pl
from jax.experimental.pallas import tpu as pltpu
from jax.sharding import Mesh, PartitionSpec as P

PANEL = 128
BOTH = 2 * PANEL
F32 = jnp.float32
BF16 = jnp.bfloat16
NT = (((1,), (1,)), ((), ()))
NN = (((1,), (0,)), ((), ()))
TN = (((0,), (0,)), ((), ()))


def split(value):
    high = value.astype(BF16)
    low = (value - high.astype(F32)).astype(BF16)
    return high, low


def dot(first, second, dims):
    return lax.dot_general(first, second, dims, preferred_element_type=F32)


def dot_split(first, second, dims):
    return (
        dot(first[0], second[1], dims)
        + dot(first[1], second[0], dims)
        + dot(first[0], second[0], dims)
    )


def dot_full(first, second, dims):
    return lax.dot_general(
        first, second, dims, precision=lax.Precision.HIGHEST, preferred_element_type=F32
    )


def square(value):
    return value * value


def cholesky_inverse(matrix):
    slabs = PANEL // 8
    lanes = lax.broadcasted_iota(jnp.int32, (8, PANEL), 1)
    sublanes = lax.broadcasted_iota(jnp.int32, (8, PANEL), 0)
    left = [matrix[8 * s : 8 * s + 8, :] for s in range(slabs)]
    right = [(lanes == sublanes + 8 * s).astype(F32) for s in range(slabs)]
    for k in range(PANEL):
        own, at = divmod(k, 8)
        row = left[own][at : at + 1, :]
        scale = lax.rsqrt(jnp.broadcast_to(row[:, k : k + 1], (1, PANEL)))
        row = jnp.broadcast_to(row * scale, (8, PANEL))
        made = jnp.broadcast_to(right[own][at : at + 1, :] * scale, (8, PANEL))
        scale = jnp.broadcast_to(scale, (8, PANEL))
        for s in range(own, slabs):
            factor = jnp.broadcast_to(left[s][:, k : k + 1], (8, PANEL)) * scale
            if s == own:
                factor = jnp.where(sublanes > at, factor, 0.0)
            left[s] = left[s] - factor * row
            kept = right[s] - factor * made
            right[s] = jnp.where(sublanes == at, made, kept) if s == own else kept
    return jnp.concatenate(right, axis=0)


def store_tile(ref, value):
    ref[0] = value[:, :PANEL]
    ref[1] = value[:, PANEL:]


def load_tile(ref):
    return jnp.concatenate([ref[0], ref[1]], axis=1)


def gram_kernel(scale, rows_ref, panel_ref, gram_ref, high_ref, low_ref):
    high, low = split(square(dot(panel_ref[...], rows_ref[...], NT)))
    high_ref[...] = high
    low_ref[...] = low
    store_tile(gram_ref, dot_split((high, low), (high, low), NT) * scale)


def sums_kernel(scale, high_ref, low_ref, rows_ref, points_ref, sums_ref):
    kernel = split(square(dot(points_ref[...], rows_ref[...], NT)))
    store_tile(sums_ref, dot_split((high_ref[...], low_ref[...]), kernel, NT) * scale)


def factor_kernel(gram_ref, rows_ref, panel_ref, q_ref, inverse_ref, high_ref, low_ref):
    gram = load_tile(gram_ref)
    first = cholesky_inverse(gram[:PANEL, :PANEL])
    lower = dot_full(gram[PANEL:, :PANEL], first, NT)
    second = cholesky_inverse(gram[PANEL:, PANEL:] - dot_full(lower, lower, NT))
    corner = -dot_full(second, dot_full(lower, first, NN), NN)
    inverse_ref[:PANEL, :PANEL] = first
    inverse_ref[:PANEL, PANEL:] = jnp.zeros_like(first)
    inverse_ref[PANEL:, :PANEL] = corner
    inverse_ref[PANEL:, PANEL:] = second
    panels = split(square(dot(rows_ref[...], panel_ref[...], NT)))
    q = dot_split(panels, split(inverse_ref[...]), NT)
    q_ref[...] = q
    high, low = split(q)
    high_ref[...] = high
    low_ref[...] = low


def apply_kernel(
    inverse_ref, sums_ref, high_ref, low_ref, rows_ref, points_ref, r_ref, out_ref
):
    r_tile = dot_full(inverse_ref[...], load_tile(sums_ref), NN)
    r_ref[...] = r_tile
    kernel = square(dot(rows_ref[...], points_ref[...], NT))
    out = kernel - dot_split((high_ref[...], low_ref[...]), split(r_tile), NN)
    out_ref[...] = out.astype(BF16)


def exchange(value, axis, count):
    parts = value.reshape(count, value.shape[0] // count, PANEL)
    return jnp.sum(lax.all_to_all(parts, axis, 0, 0), axis=0)


def collect(value, axis, count):
    copies = jnp.broadcast_to(value[None], (count,) + value.shape)
    return lax.all_to_all(copies, axis, 0, 0).reshape(count * value.shape[0], PANEL)


def reduce(value, sizes):
    flat = value.reshape(-1, PANEL)
    flat = exchange(flat, "x", sizes["x"])
    flat = exchange(flat, "z", sizes["z"])
    flat = collect(flat, "z", sizes["z"])
    flat = collect(flat, "x", sizes["x"])
    return flat.reshape(value.shape)


def on_device(sizes, descriptors, points):
    rows, width = descriptors.shape
    columns = points.shape[0]
    tiles = columns // BOTH
    total_rows = rows * sizes["z"] * sizes["x"]

    mine = jnp.broadcast_to(points[None, :PANEL], (sizes["y"], PANEL, width))
    mine = lax.all_to_all(mine, "y", 0, 0)[0]
    other = lax.ppermute(mine, "c", [(0, 1), (1, 0)])
    even = lax.axis_index("c") == 0
    panel = jnp.concatenate([jnp.where(even, mine, other), jnp.where(even, other, mine)], axis=0)

    scale = 1.0 / total_rows
    whole = pl.BlockSpec(memory_space=pltpu.VMEM)
    gram, high, low = pl.pallas_call(
        functools.partial(gram_kernel, scale),
        in_specs=[whole] * 2,
        out_specs=(whole,) * 3,
        out_shape=(
            jax.ShapeDtypeStruct((2, BOTH, PANEL), F32),
            jax.ShapeDtypeStruct((BOTH, rows), BF16),
            jax.ShapeDtypeStruct((BOTH, rows), BF16),
        ),
        name="gram",
    )(descriptors, panel)

    def fixed(*shape):
        return pl.BlockSpec(shape, lambda t: (0,) * len(shape))

    tile_spec = pl.BlockSpec((2, BOTH, PANEL), lambda t: (t, 0, 0))
    points_spec = pl.BlockSpec((BOTH, width), lambda t: (t, 0))
    sums = pl.pallas_call(
        functools.partial(sums_kernel, scale),
        grid=(tiles,),
        in_specs=[fixed(BOTH, rows), fixed(BOTH, rows), fixed(rows, width), points_spec],
        out_specs=tile_spec,
        out_shape=jax.ShapeDtypeStruct((2 * tiles, BOTH, PANEL), F32),
        name="sums",
    )(high, low, descriptors, points)

    gram = reduce(gram, sizes)
    sums = reduce(sums, sizes)

    q, inverse, high, low = pl.pallas_call(
        factor_kernel,
        in_specs=[whole] * 3,
        out_specs=(whole,) * 4,
        out_shape=(
            jax.ShapeDtypeStruct((rows, BOTH), F32),
            jax.ShapeDtypeStruct((BOTH, BOTH), F32),
            jax.ShapeDtypeStruct((rows, BOTH), BF16),
            jax.ShapeDtypeStruct((rows, BOTH), BF16),
        ),
        cost_estimate=pl.CostEstimate(flops=30_000_000_000, transcendentals=0, bytes_accessed=4_000_000),
        name="factor",
    )(gram, descriptors, panel)

    r, trailing = pl.pallas_call(
        apply_kernel,
        grid=(tiles,),
        in_specs=[
            fixed(BOTH, BOTH),
            tile_spec,
            fixed(rows, BOTH),
            fixed(rows, BOTH),
            fixed(rows, width),
            points_spec,
        ],
        out_specs=(
            pl.BlockSpec((BOTH, BOTH), lambda t: (0, t)),
            pl.BlockSpec((rows, BOTH), lambda t: (0, t)),
        ),
        out_shape=(
            jax.ShapeDtypeStruct((BOTH, columns), F32),
            jax.ShapeDtypeStruct((rows, columns), BF16),
        ),
        name="apply",
    )(inverse, sums, high, low, descriptors, points)
    return q, r, trailing


def solution(mesh):
    names = ("z", "x", "y", "c")
    fine = Mesh(mesh.devices.reshape(16, 4, 4, 2), names)
    return jax.shard_map(
        functools.partial(on_device, dict(zip(names, fine.devices.shape))),
        mesh=fine,
        in_specs=(P(("z", "x"), None), P(("y", "c"), None)),
        out_specs=(P(("z", "x"), None), P(None, ("y", "c")), P(("z", "x"), ("y", "c"))),
        check_vma=False,
    )
```

```python
import functools

import jax
import jax.numpy as jnp
from jax import lax
from jax.experimental import pallas as pl
from jax.experimental.pallas import tpu as pltpu
from jax.sharding import Mesh, PartitionSpec as P

PANEL = 128
BOTH = 2 * PANEL
F32 = jnp.float32
BF16 = jnp.bfloat16
NT = (((1,), (1,)), ((), ()))
NN = (((1,), (0,)), ((), ()))
TN = (((0,), (0,)), ((), ()))


def split(value):
    high = value.astype(BF16)
    low = (value - high.astype(F32)).astype(BF16)
    return high, low


def dot(first, second, dims):
    return lax.dot_general(first, second, dims, preferred_element_type=F32)


def dot_split(first, second, dims):
    return (
        dot(first[0], second[1], dims)
        + dot(first[1], second[0], dims)
        + dot(first[0], second[0], dims)
    )


def dot_full(first, second, dims):
    return lax.dot_general(
        first, second, dims, precision=lax.Precision.HIGHEST, preferred_element_type=F32
    )


def square(value):
    return value * value


def cholesky_inverse(matrix):
    step = 8
    slabs = PANEL // step
    lanes = lax.broadcasted_iota(jnp.int32, (step, PANEL), 1)
    sublanes = lax.broadcasted_iota(jnp.int32, (step, PANEL), 0)

    def full(value):
        return jnp.broadcast_to(value, (step, PANEL))

    left = [matrix[step * s : step * s + step, :] for s in range(slabs)]
    right = [(lanes == sublanes + step * s).astype(F32) for s in range(slabs)]
    for own in range(slabs):
        at = step * own
        columns = [full(left[own][:, at + j : at + j + 1]) for j in range(step)]
        corner = [[full(columns[j][i : i + 1, :]) for j in range(i + 1)] for i in range(step)]
        rows = [full(left[own][j : j + 1, :]) for j in range(step)]
        made = [full(right[own][j : j + 1, :]) for j in range(step)]
        scales = []
        for j in range(step):
            scale = lax.rsqrt(corner[j][j])
            scales.append(scale)
            rows[j] = rows[j] * scale
            made[j] = made[j] * scale
            for i in range(j + 1, step):
                corner[i][j] = corner[i][j] * scale
            for i in range(j + 1, step):
                for m in range(j + 1, i + 1):
                    corner[i][m] = corner[i][m] - corner[i][j] * corner[m][j]
                rows[i] = rows[i] - corner[i][j] * rows[j]
                made[i] = made[i] - corner[i][j] * made[j]
        joined = made[0]
        for j in range(1, step):
            joined = jnp.where(sublanes == j, made[j], joined)
        right[own] = joined
        for s in range(own + 1, slabs):
            factors = [full(left[s][:, at + j : at + j + 1]) for j in range(step)]
            for j in range(step):
                factors[j] = factors[j] * scales[j]
                for i in range(j + 1, step):
                    factors[i] = factors[i] - corner[i][j] * factors[j]
                left[s] = left[s] - factors[j] * rows[j]
                right[s] = right[s] - factors[j] * made[j]
    return jnp.concatenate(right, axis=0)


def store_tile(ref, value):
    ref[0] = value[:, :PANEL]
    ref[1] = value[:, PANEL:]


def load_tile(ref):
    return jnp.concatenate([ref[0], ref[1]], axis=1)


def block_kernel(rows_ref, points_ref, high_ref, low_ref):
    high, low = split(square(dot(rows_ref[...], points_ref[...], NT)))
    high_ref[...] = high
    low_ref[...] = low


def gather_kernel(
    scale, rows_ref, one_ref, two_ref, high_ref, low_ref, sums_ref, panel_high, panel_low
):
    @pl.when(pl.program_id(0) == 0)
    def _():
        points = jnp.concatenate([one_ref[...], two_ref[...]], axis=0)
        panels = split(square(dot(points, rows_ref[...], NT)))
        panel_high[...] = panels[0]
        panel_low[...] = panels[1]
        store_tile(sums_ref, dot_split(panels, panels, NT) * scale)

    @pl.when(pl.program_id(0) > 0)
    def _():
        panels = (panel_high[...], panel_low[...])
        kernel = (high_ref[...], low_ref[...])
        store_tile(sums_ref, dot_split(panels, kernel, NN) * scale)


def apply_kernel(
    gram_ref, sums_ref, rows_ref, one_ref, two_ref, high_ref, low_ref, q_ref, r_ref, out_ref,
    inverse_ref, q_high, q_low,
):
    @pl.when(pl.program_id(0) == 0)
    def _():
        points = jnp.concatenate([one_ref[...], two_ref[...]], axis=0)
        panels = split(square(dot(rows_ref[...], points, NT)))
        gram = load_tile(gram_ref)
        first = cholesky_inverse(gram[:PANEL, :PANEL])
        lower = dot_full(gram[PANEL:, :PANEL], first, NT)
        second = cholesky_inverse(gram[PANEL:, PANEL:] - dot_full(lower, lower, NT))
        corner = -dot_full(second, dot_full(lower, first, NN), NN)
        inverse_ref[:PANEL, :PANEL] = first
        inverse_ref[:PANEL, PANEL:] = jnp.zeros_like(first)
        inverse_ref[PANEL:, :PANEL] = corner
        inverse_ref[PANEL:, PANEL:] = second
        q = dot_split(panels, split(inverse_ref[...]), NT)
        q_ref[...] = q
        high, low = split(q)
        q_high[...] = high
        q_low[...] = low

    r_tile = dot_full(inverse_ref[...], load_tile(sums_ref), NN)
    r_ref[...] = r_tile
    out = dot_split((q_high[...], q_low[...]), split(r_tile), NN)
    out = (high_ref[...].astype(F32) - out) + low_ref[...].astype(F32)
    out_ref[...] = out.astype(BF16)


def exchange(value, axis, count):
    parts = value.reshape(count, value.shape[0] // count, PANEL)
    return jnp.sum(lax.all_to_all(parts, axis, 0, 0), axis=0)


def collect(value, axis, count):
    copies = jnp.broadcast_to(value[None], (count,) + value.shape)
    return lax.all_to_all(copies, axis, 0, 0).reshape(count * value.shape[0], PANEL)


def on_device(sizes, descriptors, points):
    rows, width = descriptors.shape
    columns = points.shape[0]
    tiles = columns // BOTH
    total_rows = rows * sizes["z"] * sizes["x"]

    mine = jnp.broadcast_to(points[None, :PANEL], (sizes["y"], PANEL, width))
    mine = lax.all_to_all(mine, "y", 0, 0)[0]

    def fixed(*shape):
        return pl.BlockSpec(shape, lambda t: (0,) * len(shape))

    block_spec = pl.BlockSpec((rows, BOTH), lambda t: (0, t))
    high, low = pl.pallas_call(
        block_kernel,
        grid=(tiles,),
        in_specs=[fixed(rows, width), pl.BlockSpec((BOTH, width), lambda t: (t, 0))],
        out_specs=(block_spec,) * 2,
        out_shape=(jax.ShapeDtypeStruct((rows, columns), BF16),) * 2,
        name="block",
    )(descriptors, points)

    mine, high, low = lax.optimization_barrier((mine, high, low))
    other = lax.ppermute(mine, "c", [(0, 1), (1, 0)])
    even = lax.axis_index("c") == 0
    one, two = jnp.where(even, mine, other), jnp.where(even, other, mine)

    shifted_spec = pl.BlockSpec((rows, BOTH), lambda t: (0, jnp.maximum(t - 1, 0)))
    sums = pl.pallas_call(
        functools.partial(gather_kernel, 1.0 / total_rows),
        grid=(tiles + 1,),
        in_specs=[
            fixed(rows, width),
            fixed(PANEL, width),
            fixed(PANEL, width),
            shifted_spec,
            shifted_spec,
        ],
        out_specs=pl.BlockSpec((2, BOTH, PANEL), lambda t: (t, 0, 0)),
        out_shape=jax.ShapeDtypeStruct((2 * tiles + 2, BOTH, PANEL), F32),
        scratch_shapes=[pltpu.VMEM((BOTH, rows), BF16)] * 2,
        name="gather",
    )(descriptors, one, two, high, low)

    sums = sums.reshape(-1, PANEL)
    sums = exchange(sums, "x", sizes["x"])
    sums = exchange(sums, "z", sizes["z"])
    sums = collect(sums, "z", sizes["z"])
    sums = collect(sums, "x", sizes["x"])
    sums = sums.reshape(2 * tiles + 2, BOTH, PANEL)

    return pl.pallas_call(
        apply_kernel,
        grid=(tiles,),
        in_specs=[
            fixed(2, BOTH, PANEL),
            pl.BlockSpec((2, BOTH, PANEL), lambda t: (t + 1, 0, 0)),
            fixed(rows, width),
            fixed(PANEL, width),
            fixed(PANEL, width),
            block_spec,
            block_spec,
        ],
        out_specs=(
            fixed(rows, BOTH),
            pl.BlockSpec((BOTH, BOTH), lambda t: (0, t)),
            block_spec,
        ),
        out_shape=(
            jax.ShapeDtypeStruct((rows, BOTH), F32),
            jax.ShapeDtypeStruct((BOTH, columns), F32),
            jax.ShapeDtypeStruct((rows, columns), BF16),
        ),
        scratch_shapes=[
            pltpu.VMEM((BOTH, BOTH), F32),
            pltpu.VMEM((rows, BOTH), BF16),
            pltpu.VMEM((rows, BOTH), BF16),
        ],
        name="apply",
    )(sums, sums, descriptors, one, two, high, low)


def solution(mesh):
    names = ("z", "x", "y", "c")
    fine = Mesh(mesh.devices.reshape(16, 4, 4, 2), names)
    return jax.shard_map(
        functools.partial(on_device, dict(zip(names, fine.devices.shape))),
        mesh=fine,
        in_specs=(P(("z", "x"), None), P(("y", "c"), None)),
        out_specs=(P(("z", "x"), None), P(None, ("y", "c")), P(("z", "x"), ("y", "c"))),
        check_vma=False,
    )
```

```python
import functools

import jax
import jax.numpy as jnp
from jax import lax
from jax.experimental import pallas as pl
from jax.experimental.pallas import tpu as pltpu
from jax.sharding import Mesh, PartitionSpec as P

PANEL = 128
BOTH = 2 * PANEL
F32 = jnp.float32
BF16 = jnp.bfloat16
NT = (((1,), (1,)), ((), ()))
NN = (((1,), (0,)), ((), ()))
TN = (((0,), (0,)), ((), ()))


def split(value):
    high = value.astype(BF16)
    low = (value - high.astype(F32)).astype(BF16)
    return high, low


def dot(first, second, dims):
    return lax.dot_general(first, second, dims, preferred_element_type=F32)


def dot_split(first, second, dims):
    return (
        dot(first[0], second[1], dims)
        + dot(first[1], second[0], dims)
        + dot(first[0], second[0], dims)
    )


def dot_full(first, second, dims):
    return lax.dot_general(
        first, second, dims, precision=lax.Precision.HIGHEST, preferred_element_type=F32
    )


def square(value):
    return value * value


def cholesky_inverse(matrix):
    step = 8
    slabs = PANEL // step
    lanes = lax.broadcasted_iota(jnp.int32, (step, PANEL), 1)
    sublanes = lax.broadcasted_iota(jnp.int32, (step, PANEL), 0)

    def full(value):
        return jnp.broadcast_to(value, (step, PANEL))

    left = [matrix[step * s : step * s + step, :] for s in range(slabs)]
    right = [(lanes == sublanes + step * s).astype(F32) for s in range(slabs)]
    for own in range(slabs):
        at = step * own
        columns = [full(left[own][:, at + j : at + j + 1]) for j in range(step)]
        corner = [[full(columns[j][i : i + 1, :]) for j in range(i + 1)] for i in range(step)]
        rows = [full(left[own][j : j + 1, :]) for j in range(step)]
        made = [full(right[own][j : j + 1, :]) for j in range(step)]
        scales = []
        for j in range(step):
            scale = lax.rsqrt(corner[j][j])
            scales.append(scale)
            rows[j] = rows[j] * scale
            made[j] = made[j] * scale
            for i in range(j + 1, step):
                corner[i][j] = corner[i][j] * scale
            for i in range(j + 1, step):
                for m in range(j + 1, i + 1):
                    corner[i][m] = corner[i][m] - corner[i][j] * corner[m][j]
                rows[i] = rows[i] - corner[i][j] * rows[j]
                made[i] = made[i] - corner[i][j] * made[j]
        joined = made[0]
        for j in range(1, step):
            joined = jnp.where(sublanes == j, made[j], joined)
        right[own] = joined
        for s in range(own + 1, slabs):
            factors = [full(left[s][:, at + j : at + j + 1]) for j in range(step)]
            for j in range(step):
                factors[j] = factors[j] * scales[j]
                for i in range(j + 1, step):
                    factors[i] = factors[i] - corner[i][j] * factors[j]
                left[s] = left[s] - factors[j] * rows[j]
                right[s] = right[s] - factors[j] * made[j]
    return jnp.concatenate(right, axis=0)


def store_tile(ref, value):
    ref[0] = value[:, :PANEL]
    ref[1] = value[:, PANEL:]


def load_tile(ref):
    return jnp.concatenate([ref[0], ref[1]], axis=1)


def block_kernel(rows_ref, points_ref, high_ref, low_ref):
    high, low = split(square(dot(rows_ref[...], points_ref[...], NT)))
    high_ref[...] = high
    low_ref[...] = low


def copies_kernel(points_ref, copies_ref):
    copies_ref[...] = jnp.broadcast_to(points_ref[...][None], copies_ref.shape)


def gather_kernel(
    scale, rows_ref, one_ref, two_ref, high_ref, low_ref, sums_ref, panel_ref
):
    tile = pl.program_id(0)

    @pl.when(tile == 0)
    def _():
        points = jnp.concatenate([one_ref[...], two_ref[...]], axis=0)
        high, low = split(square(dot(points, rows_ref[...], NT)))
        panel_ref[:BOTH] = high
        panel_ref[BOTH:] = low
        store_tile(sums_ref.at[pl.ds(0, 2)], dot_split((high, low), (high, low), NT) * scale)

    @pl.when(tile > 0)
    def _():
        sums = dot(panel_ref[...], high_ref[...], NN)
        sums = (sums[BOTH:] + dot(panel_ref[:BOTH], low_ref[...], NN)) + sums[:BOTH]
        store_tile(sums_ref.at[pl.ds(2 * tile, 2)], sums * scale)


def apply_kernel(
    gram_ref, sums_ref, rows_ref, one_ref, two_ref, high_ref, low_ref, q_ref, r_ref, out_ref,
    inverse_ref, q_high, q_low,
):
    @pl.when(pl.program_id(0) == 0)
    def _():
        points = jnp.concatenate([one_ref[...], two_ref[...]], axis=0)
        panels = split(square(dot(rows_ref[...], points, NT)))
        gram = load_tile(gram_ref)
        first = cholesky_inverse(gram[:PANEL, :PANEL])
        lower = dot_full(gram[PANEL:, :PANEL], first, NT)
        second = cholesky_inverse(gram[PANEL:, PANEL:] - dot_full(lower, lower, NT))
        corner = -dot_full(second, dot_full(lower, first, NN), NN)
        inverse_ref[:PANEL, :PANEL] = first
        inverse_ref[:PANEL, PANEL:] = jnp.zeros_like(first)
        inverse_ref[PANEL:, :PANEL] = corner
        inverse_ref[PANEL:, PANEL:] = second
        q = dot_split(panels, split(inverse_ref[...]), NT)
        q_ref[...] = q
        high, low = split(q)
        q_high[...] = high
        q_low[...] = low

    r_tile = dot_full(inverse_ref[...], load_tile(sums_ref), NN)
    r_ref[...] = r_tile
    out = dot_split((q_high[...], q_low[...]), split(r_tile), NN)
    out = (high_ref[...].astype(F32) - out) + low_ref[...].astype(F32)
    out_ref[...] = out.astype(BF16)


def exchange(value, axis, count):
    parts = value.reshape(count, value.shape[0] // count, PANEL)
    return jnp.sum(lax.all_to_all(parts, axis, 0, 0), axis=0)


def collect(value, axis, count):
    copies = jnp.broadcast_to(value[None], (count,) + value.shape)
    return lax.all_to_all(copies, axis, 0, 0).reshape(count * value.shape[0], PANEL)


def on_device(sizes, descriptors, points):
    rows, width = descriptors.shape
    columns = points.shape[0]
    tiles = columns // BOTH
    total_rows = rows * sizes["z"] * sizes["x"]

    whole = pl.BlockSpec(memory_space=pltpu.VMEM)
    mine = pl.pallas_call(
        copies_kernel,
        grid=(1,),
        in_specs=[pl.BlockSpec((PANEL, width), lambda t: (0, 0))],
        out_specs=whole,
        out_shape=pltpu.VMEM((sizes["y"], PANEL, width), BF16),
        name="copies",
    )(points)
    mine = lax.all_to_all(mine, "y", 0, 0)[0]

    def fixed(*shape):
        return pl.BlockSpec(shape, lambda t: (0,) * len(shape))

    block_spec = pl.BlockSpec((rows, BOTH), lambda t: (0, t))
    high, low = pl.pallas_call(
        block_kernel,
        grid=(tiles,),
        in_specs=[fixed(rows, width), pl.BlockSpec((BOTH, width), lambda t: (t, 0))],
        out_specs=(block_spec,) * 2,
        out_shape=(jax.ShapeDtypeStruct((rows, columns), BF16),) * 2,
        name="block",
    )(descriptors, points)

    mine, high, low = lax.optimization_barrier((mine, high, low))
    other = lax.ppermute(mine, "c", [(0, 1), (1, 0)])
    even = lax.axis_index("c") == 0
    one, two = jnp.where(even, mine, other), jnp.where(even, other, mine)

    shifted_spec = pl.BlockSpec((rows, BOTH), lambda t: (0, jnp.maximum(t - 1, 0)))
    sums = pl.pallas_call(
        functools.partial(gather_kernel, 1.0 / total_rows),
        grid=(tiles + 1,),
        in_specs=[
            fixed(rows, width),
            fixed(PANEL, width),
            fixed(PANEL, width),
            shifted_spec,
            shifted_spec,
        ],
        out_specs=whole,
        out_shape=pltpu.VMEM((2 * tiles + 2, BOTH, PANEL), F32),
        scratch_shapes=[pltpu.VMEM((2 * BOTH, rows), BF16)],
        name="gather",
    )(descriptors, one, two, high, low)

    sums = sums.reshape(-1, PANEL)
    sums = exchange(sums, "x", sizes["x"])
    sums = exchange(sums, "z", sizes["z"])
    sums = collect(sums, "z", sizes["z"])
    sums = collect(sums, "x", sizes["x"])
    sums = sums.reshape(2 * tiles + 2, BOTH, PANEL)

    return pl.pallas_call(
        apply_kernel,
        grid=(tiles,),
        in_specs=[
            fixed(2, BOTH, PANEL),
            pl.BlockSpec((2, BOTH, PANEL), lambda t: (t + 1, 0, 0)),
            fixed(rows, width),
            fixed(PANEL, width),
            fixed(PANEL, width),
            block_spec,
            block_spec,
        ],
        out_specs=(
            fixed(rows, BOTH),
            pl.BlockSpec((BOTH, BOTH), lambda t: (0, t)),
            block_spec,
        ),
        out_shape=(
            jax.ShapeDtypeStruct((rows, BOTH), F32),
            jax.ShapeDtypeStruct((BOTH, columns), F32),
            jax.ShapeDtypeStruct((rows, columns), BF16),
        ),
        scratch_shapes=[
            pltpu.VMEM((BOTH, BOTH), F32),
            pltpu.VMEM((rows, BOTH), BF16),
            pltpu.VMEM((rows, BOTH), BF16),
        ],
        name="apply",
    )(sums, sums, descriptors, one, two, high, low)


def solution(mesh):
    names = ("z", "x", "y", "c")
    fine = Mesh(mesh.devices.reshape(16, 4, 4, 2), names)
    return jax.shard_map(
        functools.partial(on_device, dict(zip(names, fine.devices.shape))),
        mesh=fine,
        in_specs=(P(("z", "x"), None), P(("y", "c"), None)),
        out_specs=(P(("z", "x"), None), P(None, ("y", "c")), P(("z", "x"), ("y", "c"))),
        check_vma=False,
    )
```

```python
import functools

import jax
import jax.numpy as jnp
from jax import lax
from jax.experimental import pallas as pl
from jax.experimental.pallas import tpu as pltpu
from jax.sharding import Mesh, PartitionSpec as P

PANEL = 128
BOTH = 2 * PANEL
F32 = jnp.float32
BF16 = jnp.bfloat16
NT = (((1,), (1,)), ((), ()))
NN = (((1,), (0,)), ((), ()))
TN = (((0,), (0,)), ((), ()))


def split(value):
    high = value.astype(BF16)
    low = (value - high.astype(F32)).astype(BF16)
    return high, low


def dot(first, second, dims):
    return lax.dot_general(first, second, dims, preferred_element_type=F32)


def dot_split(first, second, dims):
    return (
        dot(first[0], second[1], dims)
        + dot(first[1], second[0], dims)
        + dot(first[0], second[0], dims)
    )


def dot_full(first, second, dims):
    return lax.dot_general(
        first, second, dims, precision=lax.Precision.HIGHEST, preferred_element_type=F32
    )


def square(value):
    return value * value


def cholesky_inverse(matrix):
    step = 8
    slabs = PANEL // step
    lanes = lax.broadcasted_iota(jnp.int32, (step, PANEL), 1)
    sublanes = lax.broadcasted_iota(jnp.int32, (step, PANEL), 0)

    def full(value):
        return jnp.broadcast_to(value, (step, PANEL))

    left = [matrix[step * s : step * s + step, :] for s in range(slabs)]
    right = [(lanes == sublanes + step * s).astype(F32) for s in range(slabs)]
    for own in range(slabs):
        at = step * own
        columns = [full(left[own][:, at + j : at + j + 1]) for j in range(step)]
        corner = [[full(columns[j][i : i + 1, :]) for j in range(i + 1)] for i in range(step)]
        rows = [full(left[own][j : j + 1, :]) for j in range(step)]
        made = [full(right[own][j : j + 1, :]) for j in range(step)]
        scales = []
        for j in range(step):
            scale = lax.rsqrt(corner[j][j])
            scales.append(scale)
            rows[j] = rows[j] * scale
            made[j] = made[j] * scale
            for i in range(j + 1, step):
                corner[i][j] = corner[i][j] * scale
            for i in range(j + 1, step):
                for m in range(j + 1, i + 1):
                    corner[i][m] = corner[i][m] - corner[i][j] * corner[m][j]
                rows[i] = rows[i] - corner[i][j] * rows[j]
                made[i] = made[i] - corner[i][j] * made[j]
        joined = made[0]
        for j in range(1, step):
            joined = jnp.where(sublanes == j, made[j], joined)
        right[own] = joined
        for s in range(own + 1, slabs):
            factors = [full(left[s][:, at + j : at + j + 1]) for j in range(step)]
            for j in range(step):
                factors[j] = factors[j] * scales[j]
                for i in range(j + 1, step):
                    factors[i] = factors[i] - corner[i][j] * factors[j]
                left[s] = left[s] - factors[j] * rows[j]
                right[s] = right[s] - factors[j] * made[j]
    return jnp.concatenate(right, axis=0)


def block_kernel(rows_ref, points_ref, high_ref, low_ref):
    high, low = split(square(dot(rows_ref[...], points_ref[...], NT)))
    high_ref[...] = high
    low_ref[...] = low


def copies_kernel(points_ref, copies_ref):
    copies_ref[...] = jnp.broadcast_to(points_ref[...][None], copies_ref.shape)


def gather_kernel(
    scale, columns, rows_ref, one_ref, two_ref, high_ref, low_ref, sums_ref, panel_ref
):
    tile = pl.program_id(0)

    @pl.when(tile == 0)
    def _():
        points = jnp.concatenate([one_ref[...], two_ref[...]], axis=0)
        high, low = split(square(dot(points, rows_ref[...], NT)))
        panel_ref[:BOTH] = high
        panel_ref[BOTH:] = low
        gram = dot_split((high, low), (high, low), NT) * scale
        sums_ref[2 * columns : 2 * columns + BOTH] = gram[:, :PANEL]
        sums_ref[2 * columns + BOTH :] = gram[PANEL:, PANEL:]

    @pl.when(tile > 0)
    def _():
        sums = dot(panel_ref[...], high_ref[...], NN)
        sums = (sums[BOTH:] + dot(panel_ref[:BOTH], low_ref[...], NN)) + sums[:BOTH]
        start = pl.multiple_of((tile - 1) * 2 * BOTH, 2 * BOTH)
        sums_ref[pl.ds(start, BOTH)] = sums[:, :PANEL] * scale
        sums_ref[pl.ds(start + BOTH, BOTH)] = sums[:, PANEL:] * scale


def panels_kernel(rows_ref, one_ref, two_ref, high_ref, low_ref):
    points = jnp.concatenate([one_ref[...], two_ref[...]], axis=0)
    high, low = split(square(dot(rows_ref[...], points, NT)))
    high_ref[...] = high
    low_ref[...] = low


def apply_kernel(
    top_ref, left_ref, right_ref, sums_ref, panel_high, panel_low, high_ref, low_ref, q_ref, r_ref, out_ref,
    inverse_ref, q_high, q_low,
):
    @pl.when(pl.program_id(0) == 0)
    def _():
        panels = (panel_high[...], panel_low[...])
        first = cholesky_inverse(top_ref[...])
        lower = dot_full(left_ref[...], first, NT)
        second = cholesky_inverse(right_ref[...] - dot_full(lower, lower, NT))
        corner = -dot_full(second, dot_full(lower, first, NN), NN)
        inverse_ref[:PANEL, :PANEL] = first
        inverse_ref[:PANEL, PANEL:] = jnp.zeros_like(first)
        inverse_ref[PANEL:, :PANEL] = corner
        inverse_ref[PANEL:, PANEL:] = second
        q = dot_split(panels, split(inverse_ref[...]), NT)
        q_ref[...] = q
        high, low = split(q)
        q_high[...] = high
        q_low[...] = low

    sums = jnp.concatenate([sums_ref[:BOTH], sums_ref[BOTH:]], axis=1)
    r_tile = dot_full(inverse_ref[...], sums, NN)
    r_ref[...] = r_tile
    out = dot_split((q_high[...], q_low[...]), split(r_tile), NN)
    out = (high_ref[...].astype(F32) - out) + low_ref[...].astype(F32)
    out_ref[...] = out.astype(BF16)


def exchange(value, axis, count):
    parts = value.reshape(count, value.shape[0] // count, PANEL)
    return jnp.sum(lax.all_to_all(parts, axis, 0, 0), axis=0)


def spread(value, axis, count):
    copies = jnp.broadcast_to(value[None], (count,) + value.shape)
    return lax.all_to_all(copies, axis, 0, 0)


def collect(value, axis, count):
    return spread(value, axis, count).reshape(count * value.shape[0], PANEL)


def on_device(sizes, descriptors, points):
    rows, width = descriptors.shape
    columns = points.shape[0]
    tiles = columns // BOTH
    total_rows = rows * sizes["far"] * sizes["near"] * sizes["x"]

    whole = pl.BlockSpec(memory_space=pltpu.VMEM)
    mine = pl.pallas_call(
        copies_kernel,
        grid=(1,),
        in_specs=[pl.BlockSpec((PANEL, width), lambda t: (0, 0))],
        out_specs=whole,
        out_shape=pltpu.VMEM((sizes["y"], PANEL, width), BF16),
        name="copies",
    )(points)
    mine = lax.all_to_all(mine, "y", 0, 0)[0]

    def fixed(*shape):
        return pl.BlockSpec(shape, lambda t: (0,) * len(shape))

    block_spec = pl.BlockSpec((rows, BOTH), lambda t: (0, t))
    high, low = pl.pallas_call(
        block_kernel,
        grid=(tiles,),
        in_specs=[fixed(rows, width), pl.BlockSpec((BOTH, width), lambda t: (t, 0))],
        out_specs=(block_spec,) * 2,
        out_shape=(jax.ShapeDtypeStruct((rows, columns), BF16),) * 2,
        name="block",
    )(descriptors, points)

    mine, high, low = lax.optimization_barrier((mine, high, low))
    other = lax.ppermute(mine, "c", [(0, 1), (1, 0)])
    even = lax.axis_index("c") == 0
    one, two = jnp.where(even, mine, other), jnp.where(even, other, mine)

    shifted_spec = pl.BlockSpec((rows, BOTH), lambda t: (0, jnp.maximum(t - 1, 0)))
    sums = pl.pallas_call(
        functools.partial(gather_kernel, 1.0 / total_rows, columns),
        grid=(tiles + 1,),
        in_specs=[
            fixed(rows, width),
            fixed(PANEL, width),
            fixed(PANEL, width),
            shifted_spec,
            shifted_spec,
        ],
        out_specs=whole,
        out_shape=pltpu.VMEM((2 * columns + BOTH + PANEL, PANEL), F32),
        scratch_shapes=[pltpu.VMEM((2 * BOTH, rows), BF16)],
        name="gather",
    )(descriptors, one, two, high, low)

    sums = exchange(sums, "x", sizes["x"])
    sums = exchange(sums, "near", sizes["near"])
    parts = spread(sums, "far", sizes["far"])
    panel_high, panel_low = pl.pallas_call(
        panels_kernel,
        in_specs=[whole] * 3,
        out_specs=(whole,) * 2,
        out_shape=(jax.ShapeDtypeStruct((rows, BOTH), BF16),) * 2,
        name="panels",
    )(descriptors, one, two)
    parts, panel_high, panel_low = lax.optimization_barrier((parts, panel_high, panel_low))
    sums = jnp.sum(parts, axis=0)
    sums = collect(sums, "near", sizes["near"])
    sums = collect(sums, "x", sizes["x"])

    def gram_spec(block):
        return pl.BlockSpec((PANEL, PANEL), lambda t: (2 * columns // PANEL + block, 0))

    return pl.pallas_call(
        apply_kernel,
        grid=(tiles,),
        in_specs=[
            gram_spec(0),
            gram_spec(1),
            gram_spec(2),
            pl.BlockSpec((2 * BOTH, PANEL), lambda t: (t, 0)),
            fixed(rows, BOTH),
            fixed(rows, BOTH),
            block_spec,
            block_spec,
        ],
        out_specs=(
            fixed(rows, BOTH),
            pl.BlockSpec((BOTH, BOTH), lambda t: (0, t)),
            block_spec,
        ),
        out_shape=(
            jax.ShapeDtypeStruct((rows, BOTH), F32),
            jax.ShapeDtypeStruct((BOTH, columns), F32),
            jax.ShapeDtypeStruct((rows, columns), BF16),
        ),
        scratch_shapes=[
            pltpu.VMEM((BOTH, BOTH), F32),
            pltpu.VMEM((rows, BOTH), BF16),
            pltpu.VMEM((rows, BOTH), BF16),
        ],
        name="apply",
    )(sums, sums, sums, sums, panel_high, panel_low, high, low)


def solution(mesh):
    names = ("far", "near", "x", "y", "c")
    fine = Mesh(mesh.devices.reshape(4, 4, 4, 4, 2), names)
    rows, columns = ("far", "near", "x"), ("y", "c")
    return jax.shard_map(
        functools.partial(on_device, dict(zip(names, fine.devices.shape))),
        mesh=fine,
        in_specs=(P(rows, None), P(columns, None)),
        out_specs=(P(rows, None), P(None, columns), P(rows, columns)),
        check_vma=False,
    )
```

```python
import functools

import jax
import jax.numpy as jnp
from jax import lax
from jax.experimental import pallas as pl
from jax.experimental.pallas import tpu as pltpu
from jax.sharding import Mesh, PartitionSpec as P

PANEL = 128
BOTH = 2 * PANEL
F32 = jnp.float32
BF16 = jnp.bfloat16
NT = (((1,), (1,)), ((), ()))
NN = (((1,), (0,)), ((), ()))
TN = (((0,), (0,)), ((), ()))


def split(value):
    high = value.astype(BF16)
    low = (value - high.astype(F32)).astype(BF16)
    return high, low


def split_three(value):
    high = value.astype(BF16)
    middle, low = split(value - high.astype(F32))
    return high, middle, low


def dot(first, second, dims):
    return lax.dot_general(first, second, dims, preferred_element_type=F32)


def dot_split(first, second, dims):
    return (
        dot(first[0], second[1], dims)
        + dot(first[1], second[0], dims)
        + dot(first[0], second[0], dims)
    )


def dot_full(first, second, dims):
    return lax.dot_general(
        first, second, dims, precision=lax.Precision.HIGHEST, preferred_element_type=F32
    )


def square(value):
    return value * value


def cholesky_inverse(matrix):
    step = 8
    slabs = PANEL // step
    lanes = lax.broadcasted_iota(jnp.int32, (step, PANEL), 1)
    sublanes = lax.broadcasted_iota(jnp.int32, (step, PANEL), 0)

    def full(value):
        return jnp.broadcast_to(value, (step, PANEL))

    left = [matrix[step * s : step * s + step, :] for s in range(slabs)]
    right = [(lanes == sublanes + step * s).astype(F32) for s in range(slabs)]
    for own in range(slabs):
        at = step * own
        columns = [full(left[own][:, at + j : at + j + 1]) for j in range(step)]
        corner = [[full(columns[j][i : i + 1, :]) for j in range(i + 1)] for i in range(step)]
        rows = [full(left[own][j : j + 1, :]) for j in range(step)]
        made = [full(right[own][j : j + 1, :]) for j in range(step)]
        scales = []
        for j in range(step):
            scale = lax.rsqrt(corner[j][j])
            scales.append(scale)
            rows[j] = rows[j] * scale
            made[j] = made[j] * scale
            for i in range(j + 1, step):
                corner[i][j] = corner[i][j] * scale
            for i in range(j + 1, step):
                for m in range(j + 1, i + 1):
                    corner[i][m] = corner[i][m] - corner[i][j] * corner[m][j]
                rows[i] = rows[i] - corner[i][j] * rows[j]
                made[i] = made[i] - corner[i][j] * made[j]
        joined = made[0]
        for j in range(1, step):
            joined = jnp.where(sublanes == j, made[j], joined)
        right[own] = joined
        for s in range(own + 1, slabs):
            factors = [full(left[s][:, at + j : at + j + 1]) for j in range(step)]
            for j in range(step):
                factors[j] = factors[j] * scales[j]
                for i in range(j + 1, step):
                    factors[i] = factors[i] - corner[i][j] * factors[j]
                left[s] = left[s] - factors[j] * rows[j]
                right[s] = right[s] - factors[j] * made[j]
    return jnp.concatenate(right, axis=0)


def block_kernel(rows_ref, points_ref, high_ref, low_ref):
    high, low = split(square(dot(rows_ref[...], points_ref[...], NT)))
    high_ref[...] = high
    low_ref[...] = low


def copies_kernel(points_ref, copies_ref):
    copies_ref[...] = jnp.broadcast_to(points_ref[...][None], copies_ref.shape)


def gather_kernel(
    scale, columns, rows_ref, one_ref, two_ref, high_far, low_far, sums_ref,
    panel_ref, high_ref, low_ref, loads,
):
    tile = pl.program_id(0)

    def fetches(at):
        return (
            pltpu.make_async_copy(high_far.at[at], high_ref.at[at], loads.at[0, at]),
            pltpu.make_async_copy(low_far.at[at], low_ref.at[at], loads.at[1, at]),
        )

    @pl.when(tile == 0)
    def _():
        for at in range(high_far.shape[0]):
            for fetch in fetches(at):
                fetch.start()
        points = jnp.concatenate([one_ref[...], two_ref[...]], axis=0)
        high, low = split(square(dot(points, rows_ref[...], NT)))
        panel_ref[:BOTH] = high
        panel_ref[BOTH:] = low
        gram = dot_split((high, low), (high, low), NT) * scale
        sums_ref[2 * columns : 2 * columns + BOTH] = gram[:, :PANEL]
        sums_ref[2 * columns + BOTH :] = gram[PANEL:, PANEL:]

    @pl.when(tile > 0)
    def _():
        at = tile - 1
        for fetch in fetches(at):
            fetch.wait()
        sums = dot(panel_ref[...], high_ref[at], NN)
        sums = (sums[BOTH:] + dot(panel_ref[:BOTH], low_ref[at], NN)) + sums[:BOTH]
        start = pl.multiple_of(at * 2 * BOTH, 2 * BOTH)
        sums_ref[pl.ds(start, BOTH)] = sums[:, :PANEL] * scale
        sums_ref[pl.ds(start + BOTH, BOTH)] = sums[:, PANEL:] * scale


def panels_kernel(rows_ref, one_ref, two_ref, high_ref, low_ref):
    points = jnp.concatenate([one_ref[...], two_ref[...]], axis=0)
    high, low = split(square(dot(rows_ref[...], points, NT)))
    high_ref[...] = high
    low_ref[...] = low


def apply_kernel(
    top_ref, left_ref, right_ref, sums_ref, panel_high, panel_low, high_ref, low_ref, q_ref, r_ref, out_ref,
    parts_ref, q_high, q_low,
):
    @pl.when(pl.program_id(0) == 0)
    def _():
        panels = (panel_high[...], panel_low[...])
        first = cholesky_inverse(top_ref[...])
        lower = dot_full(left_ref[...], first, NT)
        second = cholesky_inverse(right_ref[...] - dot_full(lower, lower, NT))
        corner = -dot_full(second, dot_full(lower, first, NN), NN)
        inverse = jnp.concatenate(
            [
                jnp.concatenate([first, jnp.zeros_like(first)], axis=1),
                jnp.concatenate([corner, second], axis=1),
            ],
            axis=0,
        )
        parts = split_three(inverse)
        for at, part in enumerate(parts):
            parts_ref[at * BOTH : at * BOTH + BOTH] = part
        q = dot_split(panels, parts[:2], NT)
        q_ref[...] = q
        high, low = split(q)
        q_high[...] = high
        q_low[...] = low

    sums = jnp.concatenate([sums_ref[:BOTH], sums_ref[BOTH:]], axis=1)
    high, middle, low = split_three(sums)
    one = dot(parts_ref[...], high, NN)
    two = dot(parts_ref[: 2 * BOTH], middle, NN)
    three = dot(parts_ref[:BOTH], low, NN)
    small = (one[2 * BOTH :] + two[BOTH:]) + three
    r_tile = (small + (one[BOTH : 2 * BOTH] + two[:BOTH])) + one[:BOTH]
    r_ref[...] = r_tile
    out = dot_split((q_high[...], q_low[...]), split(r_tile), NN)
    out = (high_ref[...].astype(F32) - out) + low_ref[...].astype(F32)
    out_ref[...] = out.astype(BF16)


def exchange(value, axis, count):
    parts = value.reshape(count, value.shape[0] // count, PANEL)
    return jnp.sum(lax.all_to_all(parts, axis, 0, 0), axis=0)


def spread(value, axis, count):
    copies = jnp.broadcast_to(value[None], (count,) + value.shape)
    return lax.all_to_all(copies, axis, 0, 0)


def collect(value, axis, count):
    return spread(value, axis, count).reshape(count * value.shape[0], PANEL)


def on_device(sizes, descriptors, points):
    rows, width = descriptors.shape
    columns = points.shape[0]
    tiles = columns // BOTH
    total_rows = rows * sizes["far"] * sizes["near"] * sizes["x"]

    whole = pl.BlockSpec(memory_space=pltpu.VMEM)
    mine = pl.pallas_call(
        copies_kernel,
        grid=(1,),
        in_specs=[pl.BlockSpec((PANEL, width), lambda t: (0, 0))],
        out_specs=whole,
        out_shape=pltpu.VMEM((sizes["y"], PANEL, width), BF16),
        name="copies",
    )(points)
    mine = lax.all_to_all(mine, "y", 0, 0)[0]

    def fixed(*shape):
        return pl.BlockSpec(shape, lambda t: (0,) * len(shape))

    tile_spec = pl.BlockSpec((None, rows, BOTH), lambda t: (t, 0, 0))
    tile_shape = (tiles, rows, BOTH)
    high, low = pl.pallas_call(
        block_kernel,
        grid=(tiles,),
        in_specs=[fixed(rows, width), pl.BlockSpec((BOTH, width), lambda t: (t, 0))],
        out_specs=(tile_spec, tile_spec),
        out_shape=(jax.ShapeDtypeStruct(tile_shape, BF16),) * 2,
        name="block",
    )(descriptors, points)

    mine, high, low = lax.optimization_barrier((mine, high, low))
    other = lax.ppermute(mine, "c", [(0, 1), (1, 0)])
    even = lax.axis_index("c") == 0
    one, two = jnp.where(even, mine, other), jnp.where(even, other, mine)

    anywhere = pl.BlockSpec(memory_space=pl.ANY)
    sums = pl.pallas_call(
        functools.partial(gather_kernel, 1.0 / total_rows, columns),
        grid=(tiles + 1,),
        in_specs=[
            fixed(rows, width),
            fixed(PANEL, width),
            fixed(PANEL, width),
            anywhere,
            anywhere,
        ],
        out_specs=whole,
        out_shape=pltpu.VMEM((2 * columns + BOTH + PANEL, PANEL), F32),
        scratch_shapes=[
            pltpu.VMEM((2 * BOTH, rows), BF16),
            pltpu.VMEM(tile_shape, BF16),
            pltpu.VMEM(tile_shape, BF16),
            pltpu.SemaphoreType.DMA((2, tiles)),
        ],
        name="gather",
    )(descriptors, one, two, high, low)

    sums = exchange(sums, "x", sizes["x"])
    sums = exchange(sums, "near", sizes["near"])
    parts = spread(sums, "far", sizes["far"])
    panel_high, panel_low = pl.pallas_call(
        panels_kernel,
        in_specs=[whole] * 3,
        out_specs=(whole,) * 2,
        out_shape=(jax.ShapeDtypeStruct((rows, BOTH), BF16),) * 2,
        name="panels",
    )(descriptors, one, two)
    parts, panel_high, panel_low = lax.optimization_barrier((parts, panel_high, panel_low))
    sums = jnp.sum(parts, axis=0)
    sums = collect(sums, "near", sizes["near"])
    sums = collect(sums, "x", sizes["x"])

    def gram_spec(block):
        return pl.BlockSpec((PANEL, PANEL), lambda t: (2 * columns // PANEL + block, 0))

    return pl.pallas_call(
        apply_kernel,
        grid=(tiles,),
        in_specs=[
            gram_spec(0),
            gram_spec(1),
            gram_spec(2),
            pl.BlockSpec((2 * BOTH, PANEL), lambda t: (t, 0)),
            fixed(rows, BOTH),
            fixed(rows, BOTH),
            tile_spec,
            tile_spec,
        ],
        out_specs=(
            fixed(rows, BOTH),
            pl.BlockSpec((BOTH, BOTH), lambda t: (0, t)),
            pl.BlockSpec((rows, BOTH), lambda t: (0, t)),
        ),
        out_shape=(
            jax.ShapeDtypeStruct((rows, BOTH), F32),
            jax.ShapeDtypeStruct((BOTH, columns), F32),
            jax.ShapeDtypeStruct((rows, columns), BF16),
        ),
        scratch_shapes=[
            pltpu.VMEM((3 * BOTH, BOTH), BF16),
            pltpu.VMEM((rows, BOTH), BF16),
            pltpu.VMEM((rows, BOTH), BF16),
        ],
        name="apply",
    )(sums, sums, sums, sums, panel_high, panel_low, high, low)


def solution(mesh):
    names = ("far", "near", "x", "y", "c")
    fine = Mesh(mesh.devices.reshape(4, 4, 4, 4, 2), names)
    rows, columns = ("far", "near", "x"), ("y", "c")
    return jax.shard_map(
        functools.partial(on_device, dict(zip(names, fine.devices.shape))),
        mesh=fine,
        in_specs=(P(rows, None), P(columns, None)),
        out_specs=(P(rows, None), P(None, columns), P(rows, columns)),
        check_vma=False,
    )
```

```python
import functools

import jax
import jax.numpy as jnp
from jax import lax
from jax.experimental import pallas as pl
from jax.experimental.pallas import tpu as pltpu
from jax.sharding import Mesh, PartitionSpec as P

PANEL = 128
BOTH = 2 * PANEL
F32 = jnp.float32
BF16 = jnp.bfloat16
NT = (((1,), (1,)), ((), ()))
NN = (((1,), (0,)), ((), ()))
TN = (((0,), (0,)), ((), ()))


def split(value):
    high = value.astype(BF16)
    low = (value - high.astype(F32)).astype(BF16)
    return high, low


def split_three(value):
    high = value.astype(BF16)
    middle, low = split(value - high.astype(F32))
    return high, middle, low


def dot(first, second, dims):
    return lax.dot_general(first, second, dims, preferred_element_type=F32)


def dot_split(first, second, dims):
    return (
        dot(first[0], second[1], dims)
        + dot(first[1], second[0], dims)
        + dot(first[0], second[0], dims)
    )


def dot_full(first, second, dims):
    return lax.dot_general(
        first, second, dims, precision=lax.Precision.HIGHEST, preferred_element_type=F32
    )


def square(value):
    return value * value


def cholesky_inverse(matrix):
    step = 8
    slabs = PANEL // step
    lanes = lax.broadcasted_iota(jnp.int32, (step, PANEL), 1)
    sublanes = lax.broadcasted_iota(jnp.int32, (step, PANEL), 0)

    def full(value):
        return jnp.broadcast_to(value, (step, PANEL))

    left = [matrix[step * s : step * s + step, :] for s in range(slabs)]
    right = [(lanes == sublanes + step * s).astype(F32) for s in range(slabs)]
    for own in range(slabs):
        at = step * own
        columns = [full(left[own][:, at + j : at + j + 1]) for j in range(step)]
        corner = [[full(columns[j][i : i + 1, :]) for j in range(i + 1)] for i in range(step)]
        rows = [full(left[own][j : j + 1, :]) for j in range(step)]
        made = [full(right[own][j : j + 1, :]) for j in range(step)]
        scales = []
        for j in range(step):
            scale = lax.rsqrt(corner[j][j])
            scales.append(scale)
            rows[j] = rows[j] * scale
            made[j] = made[j] * scale
            for i in range(j + 1, step):
                corner[i][j] = corner[i][j] * scale
            for i in range(j + 1, step):
                for m in range(j + 1, i + 1):
                    corner[i][m] = corner[i][m] - corner[i][j] * corner[m][j]
                rows[i] = rows[i] - corner[i][j] * rows[j]
                made[i] = made[i] - corner[i][j] * made[j]
        joined = made[0]
        for j in range(1, step):
            joined = jnp.where(sublanes == j, made[j], joined)
        right[own] = joined
        for s in range(own + 1, slabs):
            factors = [full(left[s][:, at + j : at + j + 1]) for j in range(step)]
            for j in range(step):
                factors[j] = factors[j] * scales[j]
                for i in range(j + 1, step):
                    factors[i] = factors[i] - corner[i][j] * factors[j]
                left[s] = left[s] - factors[j] * rows[j]
                right[s] = right[s] - factors[j] * made[j]
    return jnp.concatenate(right, axis=0)


def block_kernel(rows_ref, points_ref, high_ref, low_ref):
    high, low = split(square(dot(rows_ref[...], points_ref[...], NT)))
    high_ref[...] = high
    low_ref[...] = low


def copies_kernel(points_ref, copies_ref):
    copies_ref[...] = jnp.broadcast_to(points_ref[...][None], copies_ref.shape)


def gather_kernel(
    scale, columns, rows_ref, one_ref, two_ref, high_far, low_far, sums_ref,
    panel_ref, high_ref, low_ref, loads,
):
    tile = pl.program_id(0)

    def fetches(at):
        return (
            pltpu.make_async_copy(high_far.at[at], high_ref.at[at], loads.at[0, at]),
            pltpu.make_async_copy(low_far.at[at], low_ref.at[at], loads.at[1, at]),
        )

    @pl.when(tile == 0)
    def _():
        for at in range(high_far.shape[0]):
            for fetch in fetches(at):
                fetch.start()
        points = jnp.concatenate([one_ref[...], two_ref[...]], axis=0)
        high, low = split(square(dot(points, rows_ref[...], NT)))
        panel_ref[:BOTH] = high
        panel_ref[BOTH:] = low
        gram = dot_split((high, low), (high, low), NT) * scale
        sums_ref[2 * columns : 2 * columns + BOTH] = gram[:, :PANEL]
        sums_ref[2 * columns + BOTH :] = gram[PANEL:, PANEL:]

    @pl.when(tile > 0)
    def _():
        at = tile - 1
        for fetch in fetches(at):
            fetch.wait()
        sums = dot(panel_ref[...], high_ref[at], NN)
        sums = (sums[BOTH:] + dot(panel_ref[:BOTH], low_ref[at], NN)) + sums[:BOTH]
        start = pl.multiple_of(at * 2 * BOTH, 2 * BOTH)
        sums_ref[pl.ds(start, BOTH)] = sums[:, :PANEL] * scale
        sums_ref[pl.ds(start + BOTH, BOTH)] = sums[:, PANEL:] * scale


def panels_kernel(rows_ref, one_ref, two_ref, high_ref, low_ref):
    points = jnp.concatenate([one_ref[...], two_ref[...]], axis=0)
    high, low = split(square(dot(rows_ref[...], points, NT)))
    high_ref[...] = high
    low_ref[...] = low


def apply_kernel(
    top_ref, left_ref, right_ref, sums_ref, panel_high, panel_low, high_ref, low_ref, q_ref, r_ref, out_ref,
    parts_ref, q_parts,
):
    @pl.when(pl.program_id(0) == 0)
    def _():
        panels = (panel_high[...], panel_low[...])
        first = cholesky_inverse(top_ref[...])
        lower = dot_full(left_ref[...], first, NT)
        second = cholesky_inverse(right_ref[...] - dot_full(lower, lower, NT))
        corner = -dot_full(second, dot_full(lower, first, NN), NN)
        inverse = jnp.concatenate(
            [
                jnp.concatenate([first, jnp.zeros_like(first)], axis=1),
                jnp.concatenate([corner, second], axis=1),
            ],
            axis=0,
        )
        parts = split_three(inverse)
        for at, part in enumerate(parts):
            parts_ref[at * BOTH : at * BOTH + BOTH] = part
        q = dot_split(panels, parts[:2], NT)
        q_ref[...] = q
        high, low = split(q)
        q_parts[:, :BOTH] = high
        q_parts[:, BOTH : 2 * BOTH] = high
        q_parts[:, 2 * BOTH :] = low

    sums = jnp.concatenate([sums_ref[:BOTH], sums_ref[BOTH:]], axis=1)
    high, middle, low = split_three(sums)
    one = dot(parts_ref[...], high, NN)
    two = dot(parts_ref[: 2 * BOTH], middle, NN)
    three = dot(parts_ref[:BOTH], low, NN)
    small = (one[2 * BOTH :] + two[BOTH:]) + three
    r_tile = (small + (one[BOTH : 2 * BOTH] + two[:BOTH])) + one[:BOTH]
    r_ref[...] = r_tile
    r_high, r_low = split(r_tile)
    out = dot(q_parts[...], jnp.concatenate([r_high, r_low, r_high], axis=0), NN)
    out = (high_ref[...].astype(F32) - out) + low_ref[...].astype(F32)
    out_ref[...] = out.astype(BF16)


def exchange(value, axis, count):
    parts = value.reshape(count, value.shape[0] // count, PANEL)
    return jnp.sum(lax.all_to_all(parts, axis, 0, 0), axis=0)


def spread(value, axis, count):
    copies = jnp.broadcast_to(value[None], (count,) + value.shape)
    return lax.all_to_all(copies, axis, 0, 0)


def collect(value, axis, count):
    return spread(value, axis, count).reshape(count * value.shape[0], PANEL)


def on_device(sizes, descriptors, points):
    rows, width = descriptors.shape
    columns = points.shape[0]
    tiles = columns // BOTH
    total_rows = rows * sizes["far"] * sizes["near"] * sizes["x"]

    whole = pl.BlockSpec(memory_space=pltpu.VMEM)
    mine = pl.pallas_call(
        copies_kernel,
        grid=(1,),
        in_specs=[pl.BlockSpec((PANEL, width), lambda t: (0, 0))],
        out_specs=whole,
        out_shape=pltpu.VMEM((sizes["y"], PANEL, width), BF16),
        name="copies",
    )(points)
    mine = lax.all_to_all(mine, "y", 0, 0)[0]

    def fixed(*shape):
        return pl.BlockSpec(shape, lambda t: (0,) * len(shape))

    tile_spec = pl.BlockSpec((None, rows, BOTH), lambda t: (t, 0, 0))
    tile_shape = (tiles, rows, BOTH)
    high, low = pl.pallas_call(
        block_kernel,
        grid=(tiles,),
        in_specs=[fixed(rows, width), pl.BlockSpec((BOTH, width), lambda t: (t, 0))],
        out_specs=(tile_spec, tile_spec),
        out_shape=(jax.ShapeDtypeStruct(tile_shape, BF16),) * 2,
        name="block",
    )(descriptors, points)

    mine, high, low = lax.optimization_barrier((mine, high, low))
    other = lax.ppermute(mine, "c", [(0, 1), (1, 0)])
    even = lax.axis_index("c") == 0
    one, two = jnp.where(even, mine, other), jnp.where(even, other, mine)

    anywhere = pl.BlockSpec(memory_space=pl.ANY)
    sums = pl.pallas_call(
        functools.partial(gather_kernel, 1.0 / total_rows, columns),
        grid=(tiles + 1,),
        in_specs=[
            fixed(rows, width),
            fixed(PANEL, width),
            fixed(PANEL, width),
            anywhere,
            anywhere,
        ],
        out_specs=whole,
        out_shape=pltpu.VMEM((2 * columns + BOTH + PANEL, PANEL), F32),
        scratch_shapes=[
            pltpu.VMEM((2 * BOTH, rows), BF16),
            pltpu.VMEM(tile_shape, BF16),
            pltpu.VMEM(tile_shape, BF16),
            pltpu.SemaphoreType.DMA((2, tiles)),
        ],
        name="gather",
    )(descriptors, one, two, high, low)

    sums = exchange(sums, "x", sizes["x"])
    sums = exchange(sums, "near", sizes["near"])
    parts = spread(sums, "far", sizes["far"])
    panel_high, panel_low = pl.pallas_call(
        panels_kernel,
        in_specs=[whole] * 3,
        out_specs=(whole,) * 2,
        out_shape=(jax.ShapeDtypeStruct((rows, BOTH), BF16),) * 2,
        name="panels",
    )(descriptors, one, two)
    parts, panel_high, panel_low = lax.optimization_barrier((parts, panel_high, panel_low))
    sums = jnp.sum(parts, axis=0)
    sums = collect(sums, "near", sizes["near"])
    sums = collect(sums, "x", sizes["x"])

    def gram_spec(block):
        return pl.BlockSpec((PANEL, PANEL), lambda t: (2 * columns // PANEL + block, 0))

    return pl.pallas_call(
        apply_kernel,
        grid=(tiles,),
        in_specs=[
            gram_spec(0),
            gram_spec(1),
            gram_spec(2),
            pl.BlockSpec((2 * BOTH, PANEL), lambda t: (t, 0)),
            fixed(rows, BOTH),
            fixed(rows, BOTH),
            tile_spec,
            tile_spec,
        ],
        out_specs=(
            fixed(rows, BOTH),
            pl.BlockSpec((BOTH, BOTH), lambda t: (0, t)),
            pl.BlockSpec((rows, BOTH), lambda t: (0, t)),
        ),
        out_shape=(
            jax.ShapeDtypeStruct((rows, BOTH), F32),
            jax.ShapeDtypeStruct((BOTH, columns), F32),
            jax.ShapeDtypeStruct((rows, columns), BF16),
        ),
        scratch_shapes=[
            pltpu.VMEM((3 * BOTH, BOTH), BF16),
            pltpu.VMEM((rows, 3 * BOTH), BF16),
        ],
        name="apply",
    )(sums, sums, sums, sums, panel_high, panel_low, high, low)


def solution(mesh):
    names = ("far", "near", "x", "y", "c")
    fine = Mesh(mesh.devices.reshape(4, 4, 4, 4, 2), names)
    rows, columns = ("far", "near", "x"), ("y", "c")
    return jax.shard_map(
        functools.partial(on_device, dict(zip(names, fine.devices.shape))),
        mesh=fine,
        in_specs=(P(rows, None), P(columns, None)),
        out_specs=(P(rows, None), P(None, columns), P(rows, columns)),
        check_vma=False,
    )
```

```python
import functools

import jax
import jax.numpy as jnp
from jax import lax
from jax.experimental import pallas as pl
from jax.experimental.pallas import tpu as pltpu
from jax.sharding import Mesh, PartitionSpec as P

PANEL = 128
BOTH = 2 * PANEL
F32 = jnp.float32
BF16 = jnp.bfloat16
NT = (((1,), (1,)), ((), ()))
NN = (((1,), (0,)), ((), ()))
TN = (((0,), (0,)), ((), ()))


def split(value):
    high = value.astype(BF16)
    low = (value - high.astype(F32)).astype(BF16)
    return high, low


def split_three(value):
    high = value.astype(BF16)
    middle, low = split(value - high.astype(F32))
    return high, middle, low


def dot(first, second, dims):
    return lax.dot_general(first, second, dims, preferred_element_type=F32)


def dot_split(first, second, dims):
    return (
        dot(first[0], second[1], dims)
        + dot(first[1], second[0], dims)
        + dot(first[0], second[0], dims)
    )


def dot_full(first, second, dims):
    return lax.dot_general(
        first, second, dims, precision=lax.Precision.HIGHEST, preferred_element_type=F32
    )


def square(value):
    return value * value


def cholesky_inverse(matrix):
    step = 8
    slabs = PANEL // step
    lanes = lax.broadcasted_iota(jnp.int32, (step, PANEL), 1)
    sublanes = lax.broadcasted_iota(jnp.int32, (step, PANEL), 0)

    def full(value):
        return jnp.broadcast_to(value, (step, PANEL))

    left = [matrix[step * s : step * s + step, :] for s in range(slabs)]
    right = [(lanes == sublanes + step * s).astype(F32) for s in range(slabs)]
    for own in range(slabs):
        at = step * own
        columns = [full(left[own][:, at + j : at + j + 1]) for j in range(step)]
        corner = [[full(columns[j][i : i + 1, :]) for j in range(i + 1)] for i in range(step)]
        rows = [full(left[own][j : j + 1, :]) for j in range(step)]
        made = [full(right[own][j : j + 1, :]) for j in range(step)]
        scales = []
        for j in range(step):
            scale = lax.rsqrt(corner[j][j])
            scales.append(scale)
            rows[j] = rows[j] * scale
            made[j] = made[j] * scale
            for i in range(j + 1, step):
                corner[i][j] = corner[i][j] * scale
            for i in range(j + 1, step):
                for m in range(j + 1, i + 1):
                    corner[i][m] = corner[i][m] - corner[i][j] * corner[m][j]
                rows[i] = rows[i] - corner[i][j] * rows[j]
                made[i] = made[i] - corner[i][j] * made[j]
        joined = made[0]
        for j in range(1, step):
            joined = jnp.where(sublanes == j, made[j], joined)
        right[own] = joined
        for s in range(own + 1, slabs):
            factors = [full(left[s][:, at + j : at + j + 1]) for j in range(step)]
            for j in range(step):
                factors[j] = factors[j] * scales[j]
                for i in range(j + 1, step):
                    factors[i] = factors[i] - corner[i][j] * factors[j]
                left[s] = left[s] - factors[j] * rows[j]
                right[s] = right[s] - factors[j] * made[j]
    return jnp.concatenate(right, axis=0)


def block_kernel(rows_ref, points_ref, high_ref, low_ref):
    high, low = split(square(dot(rows_ref[...], points_ref[...], NT)))
    high_ref[...] = high
    low_ref[...] = low


def copies_kernel(points_ref, copies_ref, sent):
    source = points_ref.at[pl.ds(0, PANEL)]
    count = copies_ref.shape[0]
    moves = [pltpu.make_async_copy(source, copies_ref.at[i], sent.at[i]) for i in range(count)]
    for move in moves:
        move.start()
    for move in moves:
        move.wait()


def gather_kernel(
    scale, columns, rows_ref, one_ref, two_ref, high_far, low_far, sums_ref,
    panel_ref, high_ref, low_ref, loads,
):
    tile = pl.program_id(0)

    def fetches(at):
        return (
            pltpu.make_async_copy(high_far.at[at], high_ref.at[at], loads.at[0, at]),
            pltpu.make_async_copy(low_far.at[at], low_ref.at[at], loads.at[1, at]),
        )

    @pl.when(tile == 0)
    def _():
        for at in range(high_far.shape[0]):
            for fetch in fetches(at):
                fetch.start()
        points = jnp.concatenate([one_ref[...], two_ref[...]], axis=0)
        high, low = split(square(dot(points, rows_ref[...], NT)))
        panel_ref[:BOTH] = high
        panel_ref[BOTH:] = low
        gram = dot_split((high, low), (high, low), NT) * scale
        sums_ref[2 * columns : 2 * columns + BOTH] = gram[:, :PANEL]
        sums_ref[2 * columns + BOTH :] = gram[PANEL:, PANEL:]

    @pl.when(tile > 0)
    def _():
        at = tile - 1
        for fetch in fetches(at):
            fetch.wait()
        sums = dot(panel_ref[...], high_ref[at], NN)
        sums = (sums[BOTH:] + dot(panel_ref[:BOTH], low_ref[at], NN)) + sums[:BOTH]
        start = pl.multiple_of(at * 2 * BOTH, 2 * BOTH)
        sums_ref[pl.ds(start, BOTH)] = sums[:, :PANEL] * scale
        sums_ref[pl.ds(start + BOTH, BOTH)] = sums[:, PANEL:] * scale


def panels_kernel(rows_ref, one_ref, two_ref, high_ref, low_ref):
    points = jnp.concatenate([one_ref[...], two_ref[...]], axis=0)
    high, low = split(square(dot(rows_ref[...], points, NT)))
    high_ref[...] = high
    low_ref[...] = low


def apply_kernel(
    top_ref, left_ref, right_ref, sums_ref, panel_high, panel_low, high_ref, low_ref, q_ref, r_ref, out_ref,
    parts_ref, q_high, q_low,
):
    @pl.when(pl.program_id(0) == 0)
    def _():
        panels = (panel_high[...], panel_low[...])
        first = cholesky_inverse(top_ref[...])
        lower = dot_full(left_ref[...], first, NT)
        second = cholesky_inverse(right_ref[...] - dot_full(lower, lower, NT))
        corner = -dot_full(second, dot_full(lower, first, NN), NN)
        inverse = jnp.concatenate(
            [
                jnp.concatenate([first, jnp.zeros_like(first)], axis=1),
                jnp.concatenate([corner, second], axis=1),
            ],
            axis=0,
        )
        parts = split_three(inverse)
        for at, part in enumerate(parts):
            parts_ref[at * BOTH : at * BOTH + BOTH] = part
        q = dot_split(panels, parts[:2], NT)
        q_ref[...] = q
        high, low = split(q)
        q_high[...] = high
        q_low[...] = low

    sums = jnp.concatenate([sums_ref[:BOTH], sums_ref[BOTH:]], axis=1)
    high, middle, low = split_three(sums)
    one = dot(parts_ref[...], high, NN)
    two = dot(parts_ref[: 2 * BOTH], middle, NN)
    three = dot(parts_ref[:BOTH], low, NN)
    small = (one[2 * BOTH :] + two[BOTH:]) + three
    r_tile = (small + (one[BOTH : 2 * BOTH] + two[:BOTH])) + one[:BOTH]
    r_ref[...] = r_tile
    out = dot_split((q_high[...], q_low[...]), split(r_tile), NN)
    out = (high_ref[...].astype(F32) - out) + low_ref[...].astype(F32)
    out_ref[...] = out.astype(BF16)


def exchange(value, axis, count):
    parts = value.reshape(count, value.shape[0] // count, PANEL)
    return jnp.sum(lax.all_to_all(parts, axis, 0, 0), axis=0)


def spread(value, axis, count):
    copies = jnp.broadcast_to(value[None], (count,) + value.shape)
    return lax.all_to_all(copies, axis, 0, 0)


def collect(value, axis, count):
    return spread(value, axis, count).reshape(count * value.shape[0], PANEL)


def on_device(sizes, descriptors, points):
    rows, width = descriptors.shape
    columns = points.shape[0]
    tiles = columns // BOTH
    total_rows = rows * sizes["far"] * sizes["near"] * sizes["x"]

    whole = pl.BlockSpec(memory_space=pltpu.VMEM)
    mine = pl.pallas_call(
        copies_kernel,
        in_specs=[pl.BlockSpec(memory_space=pl.ANY)],
        out_specs=pl.BlockSpec(memory_space=pl.ANY),
        out_shape=jax.ShapeDtypeStruct((sizes["y"], PANEL, width), BF16),
        scratch_shapes=[pltpu.SemaphoreType.DMA((sizes["y"],))],
        name="copies",
    )(points)
    mine = lax.all_to_all(mine, "y", 0, 0)[0]

    def fixed(*shape):
        return pl.BlockSpec(shape, lambda t: (0,) * len(shape))

    tile_spec = pl.BlockSpec((None, rows, BOTH), lambda t: (t, 0, 0))
    tile_shape = (tiles, rows, BOTH)
    high, low = pl.pallas_call(
        block_kernel,
        grid=(tiles,),
        in_specs=[fixed(rows, width), pl.BlockSpec((BOTH, width), lambda t: (t, 0))],
        out_specs=(tile_spec, tile_spec),
        out_shape=(jax.ShapeDtypeStruct(tile_shape, BF16),) * 2,
        name="block",
    )(descriptors, points)

    mine, high, low = lax.optimization_barrier((mine, high, low))
    other = lax.ppermute(mine, "c", [(0, 1), (1, 0)])
    even = lax.axis_index("c") == 0
    one, two = jnp.where(even, mine, other), jnp.where(even, other, mine)

    anywhere = pl.BlockSpec(memory_space=pl.ANY)
    sums = pl.pallas_call(
        functools.partial(gather_kernel, 1.0 / total_rows, columns),
        grid=(tiles + 1,),
        in_specs=[
            fixed(rows, width),
            fixed(PANEL, width),
            fixed(PANEL, width),
            anywhere,
            anywhere,
        ],
        out_specs=whole,
        out_shape=pltpu.VMEM((2 * columns + BOTH + PANEL, PANEL), F32),
        scratch_shapes=[
            pltpu.VMEM((2 * BOTH, rows), BF16),
            pltpu.VMEM(tile_shape, BF16),
            pltpu.VMEM(tile_shape, BF16),
            pltpu.SemaphoreType.DMA((2, tiles)),
        ],
        name="gather",
    )(descriptors, one, two, high, low)

    sums = exchange(sums, "x", sizes["x"])
    sums = exchange(sums, "near", sizes["near"])
    parts = spread(sums, "far", sizes["far"])
    panel_high, panel_low = pl.pallas_call(
        panels_kernel,
        in_specs=[whole] * 3,
        out_specs=(whole,) * 2,
        out_shape=(jax.ShapeDtypeStruct((rows, BOTH), BF16),) * 2,
        name="panels",
    )(descriptors, one, two)
    parts, panel_high, panel_low = lax.optimization_barrier((parts, panel_high, panel_low))
    sums = jnp.sum(parts, axis=0)
    sums = collect(sums, "near", sizes["near"])
    sums = collect(sums, "x", sizes["x"])

    def gram_spec(block):
        return pl.BlockSpec((PANEL, PANEL), lambda t: (2 * columns // PANEL + block, 0))

    return pl.pallas_call(
        apply_kernel,
        grid=(tiles,),
        in_specs=[
            gram_spec(0),
            gram_spec(1),
            gram_spec(2),
            pl.BlockSpec((2 * BOTH, PANEL), lambda t: (t, 0)),
            fixed(rows, BOTH),
            fixed(rows, BOTH),
            tile_spec,
            tile_spec,
        ],
        out_specs=(
            fixed(rows, BOTH),
            pl.BlockSpec((BOTH, BOTH), lambda t: (0, t)),
            pl.BlockSpec((rows, BOTH), lambda t: (0, t)),
        ),
        out_shape=(
            jax.ShapeDtypeStruct((rows, BOTH), F32),
            jax.ShapeDtypeStruct((BOTH, columns), F32),
            jax.ShapeDtypeStruct((rows, columns), BF16),
        ),
        scratch_shapes=[
            pltpu.VMEM((3 * BOTH, BOTH), BF16),
            pltpu.VMEM((rows, BOTH), BF16),
            pltpu.VMEM((rows, BOTH), BF16),
        ],
        name="apply",
    )(sums, sums, sums, sums, panel_high, panel_low, high, low)


def solution(mesh):
    names = ("far", "near", "x", "y", "c")
    fine = Mesh(mesh.devices.reshape(4, 4, 4, 4, 2), names)
    rows, columns = ("far", "near", "x"), ("y", "c")
    return jax.shard_map(
        functools.partial(on_device, dict(zip(names, fine.devices.shape))),
        mesh=fine,
        in_specs=(P(rows, None), P(columns, None)),
        out_specs=(P(rows, None), P(None, columns), P(rows, columns)),
        check_vma=False,
    )
```
